256 devices in a mesh: ctx: 64 (over y_hi, z, x), head: 4 (over y_lo, core).
Axes of the slice: x: 4, y: 4 (y_hi: 2, y_lo: 2; y = y_hi * 2 + y_lo), z: 8, core: 2. Of those that a mesh axis runs over, the one named last changes fastest.
Arguments:
- queries: bfloat16 [16384, 2048], P('ctx', 'head'), may hold values from -6 to 6
- keys: bfloat16 [16384, 2048], P('ctx', 'head'), may hold values from -6 to 6
- values: bfloat16 [16384, 2048], P('ctx', 'head'), may hold values from -6 to 6
- out_weight: bfloat16 [2048, 2048], P('head'), may hold values from -0.125 to 0.125
- upstream: bfloat16 [16384, 2048], P('ctx', 'head'), may hold values from -6 to 6
- rand_round: int32 [256, 3], P('ctx'), may hold values from 0 to 3, as said below
- rand_block: int32 [256, 3], P('ctx'), may hold values from 0 to 3
Outputs:
- mixed: bfloat16 [16384, 2048], P('ctx', 'head')
- grad_queries: bfloat16 [16384, 2048], P('ctx', 'head')
- grad_keys: bfloat16 [16384, 2048], P('ctx', 'head')
- grad_values: bfloat16 [16384, 2048], P('ctx', 'head')
The draws below stay inside these ranges and needn't reach their ends.
Inputs may be any that keep to these rules, and one draw needn't show every extreme that they name: `rand_round`: the three entries of one query block name three different rounds.
All inputs are finite; a program needn't handle non-finite values.
Results may differ from the reference program's by a relative error of at most 0.023.
Values may be sent and summed in bfloat16 or wider, within the bound.
A program may use at most 64 MiB of HBM per device.

```python
import math
import jax
import jax.numpy as jnp
from jax import lax

HEADS = 16
HDIM = 128
BS = 64
BLK_DEV = 4
D = 2048
NBLOCKS = 256
TOKENS = 16384
N_CTX = 64


def base_rows(key, salt):
    return jnp.clip(jax.random.normal(jax.random.fold_in(key, salt), (TOKENS, D), jnp.float32), -6.0, 6.0)


def draw_queries(key, part):
    rows_drawn = base_rows(key, 1)
    return rows_drawn.astype(jnp.bfloat16)


def draw_keys(key, part):
    rows_drawn = base_rows(key, 2)
    return rows_drawn.astype(jnp.bfloat16)


def draw_rand_round(key, part):
    attention_logits = jax.random.randint(jax.random.fold_in(key, 7), (NBLOCKS, 4), 0, 1024) * 4 + jnp.arange(4, dtype=jnp.int32)[None, :]
    order = jnp.argsort(attention_logits, axis=1)
    return order[:, :3].astype(jnp.int32)


def place_ends(drawn, key, low, top_value):
    spot = [jax.random.randint(jax.random.fold_in(key, axis), (), 0, length) for axis, length in enumerate(drawn.shape)]
    widest = drawn.shape.index(max(drawn.shape))
    beside = spot[:widest] + [(spot[widest] + 1) % drawn.shape[widest]] + spot[widest + 1:]
    return drawn.at[tuple(spot)].set(low).at[tuple(beside)].set(top_value)


def level_of(stream_key, extent, cuts, low, top_value):
    loudness, own = 1.0, jax.random.fold_in(stream_key, 6)
    for position, shards_of in cuts:
        steps = jnp.exp(jax.random.uniform(jax.random.fold_in(own, position), (shards_of,), jnp.float32, low / len(cuts), top_value / len(cuts)))
        loudness = loudness * jnp.repeat(steps, extent[position] // shards_of).reshape([-1 if axis == position else 1 for axis in range(len(extent))])
    return loudness


def noise(stream_key, dims, scale, reach, pieces=(), held_as=jnp.bfloat16):
    loudness = level_of(stream_key, dims, pieces, -0.22, 0.18) if pieces else 1.0
    values = jax.random.normal(stream_key, dims, jnp.float32) * scale * loudness
    return jnp.minimum(jnp.maximum(values, -reach), reach).astype(held_as)


def setup_inputs(seed: int = 0) -> dict:
    arg_keys = jax.random.split(jax.random.key(seed), 8)
    return {
        "queries": draw_queries(jax.random.fold_in(arg_keys[7], 71), 0),
        "keys": draw_keys(jax.random.fold_in(arg_keys[7], 71), 0),
        "values": noise(arg_keys[2], (TOKENS, D), 1.0, 6.0, ((0, 64), (1, 4))),
        "out_weight": noise(arg_keys[3], (D, D), D ** -0.5, 0.125, ((0, 4),)),
        "upstream": noise(arg_keys[4], (TOKENS, D), 1.0, 6.0, ((0, 64), (1, 4))),
        "rand_round": draw_rand_round(jax.random.fold_in(arg_keys[7], 71), 0),
        "rand_block": place_ends(jax.random.randint(arg_keys[6], (NBLOCKS, 3), 0, BLK_DEV), jax.random.fold_in(arg_keys[6], 1), 0, BLK_DEV - 1).astype(jnp.int32),
    }


def key_lists(rand_round, rand_block):
    block_count = TOKENS // BS
    blocks = jnp.arange(block_count, dtype=jnp.int32)
    device = blocks // BLK_DEV
    offsets = jnp.array([N_CTX * factor // 8 for factor in (4, 2, 3, 5)], dtype=jnp.int32)
    partner = (device[:, None] - offsets[rand_round]) % N_CTX
    random_ids = (partner * BLK_DEV + rand_block).astype(jnp.int32)
    left = jnp.maximum(blocks - 1, 0)
    right = jnp.minimum(blocks + 1, block_count - 1)
    ids = jnp.concatenate([left[:, None], blocks[:, None], right[:, None], jnp.zeros_like(blocks)[:, None], random_ids], axis=1).astype(jnp.int32)
    allowed = jnp.concatenate([(blocks >= 1)[:, None], jnp.ones((block_count, 1), jnp.bool_), (blocks <= block_count - 2)[:, None], (blocks >= 2)[:, None], jnp.ones((block_count, 3), jnp.bool_)], axis=1)
    return (ids, allowed)

def head_probs(query_matrix, key_rows, value_rows, ids, allowed):
    logit_scale = 1.0 / math.sqrt(HDIM)
    key_bundle = key_rows[ids].astype(jnp.float32)
    value_bundle = value_rows[ids].astype(jnp.float32)
    attention_logits = jnp.einsum('lzg,lmcg->lzmc', query_matrix.astype(jnp.float32), key_bundle) * logit_scale
    attention_logits = jnp.where(allowed[:, None, :, None], attention_logits, -jnp.inf)
    row_max = lax.optimization_barrier(jnp.max(attention_logits, axis=(2, 3), keepdims=True))
    raw = jnp.exp(attention_logits - row_max)
    probs = raw / lax.optimization_barrier(jnp.sum(raw, axis=(2, 3), keepdims=True))
    return (probs, key_bundle, value_bundle)

def reference(queries, keys, values, out_weight, upstream, rand_round, rand_block):
    block_count = TOKENS // BS
    logit_scale = 1.0 / math.sqrt(HDIM)
    ids, allowed = key_lists(rand_round, rand_block)

    def split(array):
        return array.reshape(block_count, BS, HEADS, HDIM).transpose(2, 0, 1, 3)

    def merge(array):
        return array.transpose(1, 2, 0, 3).reshape(TOKENS, HEADS * HDIM)

    def forward(operands):
        query_matrix, key_rows, value_rows = operands
        probs, key_bundle, value_bundle = head_probs(query_matrix, key_rows, value_rows, ids, allowed)
        probabilities_blocked = lax.optimization_barrier(probs.astype(jnp.bfloat16)).astype(jnp.float32)
        return jnp.einsum('zwan,zanh->zwh', probabilities_blocked, value_bundle).astype(jnp.bfloat16)
    q_heads, k_heads, v_heads = (split(queries), split(keys), split(values))
    attn_heads = lax.map(forward, (q_heads, k_heads, v_heads))
    attention = merge(attn_heads)
    mixed = jnp.dot(attention, out_weight, preferred_element_type=jnp.float32).astype(jnp.bfloat16)
    grad_attention = jnp.dot(upstream, out_weight.T, preferred_element_type=jnp.float32).astype(jnp.bfloat16)
    grad_heads = split(grad_attention)

    def backward(operands):
        query_matrix, key_rows, value_rows, attn_out, grad_out = operands
        probs, key_bundle, value_bundle = head_probs(query_matrix, key_rows, value_rows, ids, allowed)
        probabilities_blocked = lax.optimization_barrier(probs.astype(jnp.bfloat16)).astype(jnp.float32)
        grad_features = grad_out.astype(jnp.float32)
        delta = lax.optimization_barrier(jnp.sum(grad_features * attn_out.astype(jnp.float32), axis=-1))
        grad_probabilities = jnp.einsum('lzg,lmcg->lzmc', grad_features, value_bundle)
        grad_logits = probs * (grad_probabilities - delta[:, :, None, None])
        grad_logits = lax.optimization_barrier(grad_logits.astype(jnp.bfloat16)).astype(jnp.float32)
        grad_query_rows = (logit_scale * jnp.einsum('zwan,zanh->zwh', grad_logits, key_bundle)).astype(jnp.bfloat16)
        partial_keys = logit_scale * jnp.einsum('xalp,xat->xlpt', grad_logits, query_matrix.astype(jnp.float32))
        partial_values = jnp.einsum('xalp,xat->xlpt', probabilities_blocked, grad_features)
        zeros = jnp.zeros((block_count, BS, HDIM), jnp.float32)
        grad_k = zeros.at[ids].add(partial_keys).astype(jnp.bfloat16)
        grad_v = zeros.at[ids].add(partial_values).astype(jnp.bfloat16)
        return (grad_query_rows, grad_k, grad_v)
    grad_query_rows, grad_k, grad_v = lax.map(backward, (q_heads, k_heads, v_heads, attn_heads, grad_heads))
    return (mixed, merge(grad_query_rows), merge(grad_k), merge(grad_v))
```

```python
import math

import jax
import jax.numpy as jnp
from jax import lax
from jax.sharding import PartitionSpec as P

HDIM = 128
BS = 64


def padded_2(block, sides, width):
    for axis, dim in sides:
        count = lax.axis_size(axis)
        forward = [(i, i + 1) for i in range(count - 1)]
        backward = [(target, source) for source, target in forward]
        low = lax.ppermute(
            lax.slice_in_dim(block, block.shape[dim] - width, None, axis=dim), axis, forward
        )
        high = lax.ppermute(lax.slice_in_dim(block, 0, width, axis=dim), axis, backward)
        block = jnp.concatenate([low, block, high], axis=dim)
    return block


def tree_strides(count, radix=4):
    strides, stride = [], 1
    while stride < count:
        strides.append((stride, min(radix, count // stride)))
        stride *= radix
    return strides


def spread_down(value, axis):
    count = lax.axis_size(axis)
    position = lax.axis_index(axis)
    for stride, ways in reversed(tree_strides(count)):
        digit = (position // stride) % ways
        arrivals = [
            lax.ppermute(
                value, axis, [(i, i + turn * stride) for i in range(0, count, stride * ways)]
            )
            for turn in range(1, ways)
        ]
        holds = position % (stride * ways) == 0
        fresh = arrivals[0]
        for turn in range(2, ways):
            fresh = jnp.where(digit == turn, arrivals[turn - 1], fresh)
        value = jnp.where(holds, value, fresh)
    return value


def sum_up(value, axis):
    count = lax.axis_size(axis)
    for stride, ways in tree_strides(count):
        sent = value.astype(jnp.bfloat16)
        for turn in range(1, ways):
            route = [(i + turn * stride, i) for i in range(0, count, stride * ways)]
            value = value + lax.ppermute(sent, axis, route).astype(jnp.float32)
    return value


def from_behind(block, axis, distance):
    devices = range(lax.axis_size(axis))
    route = [((i - distance) % len(devices), i) for i in devices]
    return lax.ppermute(block, axis, route)


def shifted(block, axis, distance):
    devices = range(lax.axis_size(axis))
    route = [(i - distance, i) for i in devices if i - distance in devices]
    return lax.ppermute(block, axis, route)


def body(queries, keys, values, out_weight, upstream, rand_round, rand_block):
    row_count, width_here = queries.shape
    head_dim = HDIM
    heads_here = width_here // head_dim
    block_rows = BS
    run_blocks = row_count // block_rows
    axis_count = lax.axis_size("ctx")
    position = lax.axis_index("ctx")
    logit_scale = 1.0 / math.sqrt(head_dim)
    offsets = [axis_count * factor // 8 for factor in (4, 2, 3, 5)]
    total_blocks = axis_count * run_blocks
    blocks = position * run_blocks + jnp.arange(run_blocks, dtype=jnp.int32)
    always = jnp.ones((run_blocks,), jnp.bool_)
    allowed = jnp.stack(
        [blocks >= 1, always, blocks <= total_blocks - 2, blocks >= 2, always, always, always],
        axis=1,
    )
    key_value = jnp.stack([keys, values])
    padded = padded_2(key_value, (("ctx", 1),), block_rows)
    framed = padded.reshape(2, run_blocks + 2, block_rows, width_here)
    window = jnp.stack(
        [framed[:, :run_blocks], framed[:, 1 : run_blocks + 1], framed[:, 2:]], axis=2
    )
    anchor = spread_down(key_value[:, :block_rows], "ctx")
    anchor_slot = jnp.broadcast_to(
        anchor[:, None, None], (2, run_blocks, 1, block_rows, width_here)
    )
    picks = (rand_round * run_blocks + rand_block).reshape(-1)

    def assemble(arrivals):
        pool = jnp.stack(arrivals, axis=1).reshape(2, 4 * run_blocks, block_rows, width_here)
        chosen = jnp.take(pool, picks, axis=1).reshape(2, run_blocks, 3, block_rows, width_here)
        return jnp.concatenate([window, anchor_slot, chosen], axis=2)

    arrivals = [from_behind(key_value, "ctx", offset) for offset in offsets]
    gathered = assemble(arrivals)
    q_blocks = queries.reshape(run_blocks, block_rows, heads_here, head_dim)
    key_bundle = gathered[0].reshape(run_blocks, 7, block_rows, heads_here, head_dim)
    value_bundle = gathered[1].reshape(run_blocks, 7, block_rows, heads_here, head_dim)
    attention_logits = (
        jnp.einsum("bqhd,bjkhd->bhqjk", q_blocks, key_bundle, preferred_element_type=jnp.float32)
        * logit_scale
    )
    attention_logits = jnp.where(allowed[:, None, None, :, None], attention_logits, -jnp.inf)
    row_max = jnp.max(attention_logits, axis=(3, 4), keepdims=True)
    raw = jnp.exp(attention_logits - row_max)
    row_total = jnp.sum(raw, axis=(3, 4), keepdims=True)
    probs = raw / row_total
    probabilities_blocked = probs.astype(jnp.bfloat16)
    attn_blocks = jnp.einsum(
        "bhqjk,bjkhd->bqhd", probabilities_blocked, value_bundle, preferred_element_type=jnp.float32
    ).astype(jnp.bfloat16)
    attention = attn_blocks.reshape(row_count, width_here)
    partial_out = jnp.dot(attention, out_weight, preferred_element_type=jnp.float32)
    mixed = lax.psum_scatter(
        partial_out.astype(jnp.bfloat16), "head", scatter_dimension=1, tiled=True
    )
    grad_attention = lax.dot_general(
        lax.all_gather(upstream, "head", axis=1, tiled=True),
        out_weight,
        (((1,), (1,)), ((), ())),
        preferred_element_type=jnp.float32,
    ).astype(jnp.bfloat16)
    grad_blocks = grad_attention.reshape(run_blocks, block_rows, heads_here, head_dim)
    delta = jnp.sum(grad_blocks.astype(jnp.float32) * attn_blocks.astype(jnp.float32), axis=-1)
    grad_probabilities = jnp.einsum(
        "bqhd,bjkhd->bhqjk", grad_blocks, value_bundle, preferred_element_type=jnp.float32
    )
    grad_logits = (probs * (grad_probabilities - delta.transpose(0, 2, 1)[..., None, None])).astype(
        jnp.bfloat16
    )
    grad_query_rows = logit_scale * jnp.einsum(
        "bhqjk,bjkhd->bqhd", grad_logits, key_bundle, preferred_element_type=jnp.float32
    )
    grad_queries = grad_query_rows.astype(jnp.bfloat16).reshape(row_count, width_here)
    slot_count = 7
    partial_keys = logit_scale * jnp.einsum(
        "bhqjk,bqhd->bjkhd", grad_logits, q_blocks, preferred_element_type=jnp.float32
    )
    partial_values = jnp.einsum(
        "bhqjk,bqhd->bjkhd", probabilities_blocked, grad_blocks, preferred_element_type=jnp.float32
    )
    parts = jnp.stack([partial_keys, partial_values]).reshape(
        2, run_blocks, slot_count, block_rows, width_here
    )
    framed_grad = jnp.zeros((2, run_blocks + 2, block_rows, width_here), jnp.float32)
    framed_grad = framed_grad.at[:, :run_blocks].add(parts[:, :, 0])
    framed_grad = framed_grad.at[:, 1 : run_blocks + 1].add(parts[:, :, 1])
    framed_grad = framed_grad.at[:, 2:].add(parts[:, :, 2])
    own_grad = framed_grad[:, 1 : run_blocks + 1]
    for step_by, rim_grad, slot_index in (
        (-1, framed_grad[:, 0], run_blocks - 1),
        (1, framed_grad[:, run_blocks + 1], 0),
    ):
        arrived = shifted(rim_grad.astype(jnp.bfloat16), "ctx", step_by).astype(rim_grad.dtype)
        own_grad = own_grad.at[:, slot_index].add(arrived)
    anchor_grad = sum_up(jnp.sum(parts[:, :, 3], axis=1), "ctx")
    own_grad = own_grad.at[:, 0].add(jnp.where(position == 0, anchor_grad, 0.0))
    random_parts = parts[:, :, 4:].reshape(2, run_blocks * 3, block_rows, width_here)
    spread = (
        jnp.zeros((2, 4 * run_blocks, block_rows, width_here), jnp.float32)
        .at[:, picks]
        .add(random_parts)
    )
    spread = spread.reshape(2, 4, run_blocks, block_rows, width_here)
    for turn_index in range(4):
        returned = from_behind(
            spread[:, turn_index].astype(jnp.bfloat16), "ctx", -offsets[turn_index]
        ).astype(jnp.float32)
        own_grad = own_grad + returned
    grad_keys = own_grad[0].reshape(row_count, width_here).astype(jnp.bfloat16)
    grad_values = own_grad[1].reshape(row_count, width_here).astype(jnp.bfloat16)
    return (mixed, grad_queries, grad_keys, grad_values)


def solution(mesh):
    placed = (
        P("ctx", "head"),
        P("ctx", "head"),
        P("ctx", "head"),
        P("head", None),
        P("ctx", "head"),
        P("ctx", None),
        P("ctx", None),
    )
    return jax.shard_map(
        body,
        mesh=mesh,
        in_specs=placed,
        out_specs=(P("ctx", "head"), P("ctx", "head"), P("ctx", "head"), P("ctx", "head")),
        check_vma=False,
    )
```

```python
import functools
import math

import jax
import jax.numpy as jnp
from jax import lax
from jax.experimental import pallas as pl
from jax.experimental.pallas import tpu as pltpu
from jax.sharding import PartitionSpec as P

HDIM = 128
BS = 64


def tree_strides(count, radix=4):
    strides, stride = [], 1
    while stride < count:
        strides.append((stride, min(radix, count // stride)))
        stride *= radix
    return strides


def spread_down(value, axis):
    count = lax.axis_size(axis)
    position = lax.axis_index(axis)
    for stride, ways in reversed(tree_strides(count)):
        digit = (position // stride) % ways
        arrivals = [
            lax.ppermute(
                value, axis, [(i, i + turn * stride) for i in range(0, count, stride * ways)]
            )
            for turn in range(1, ways)
        ]
        holds = position % (stride * ways) == 0
        fresh = arrivals[0]
        for turn in range(2, ways):
            fresh = jnp.where(digit == turn, arrivals[turn - 1], fresh)
        value = jnp.where(holds, value, fresh)
    return value


def sum_up(value, axis):
    count = lax.axis_size(axis)
    for stride, ways in tree_strides(count):
        sent = value.astype(jnp.bfloat16)
        for turn in range(1, ways):
            route = [(i + turn * stride, i) for i in range(0, count, stride * ways)]
            value = value + lax.ppermute(sent, axis, route).astype(jnp.float32)
    return value


def from_behind(block, axis, distance):
    devices = range(lax.axis_size(axis))
    route = [((i - distance) % len(devices), i) for i in devices]
    return lax.ppermute(block, axis, route)


def shifted(block, axis, distance):
    devices = range(lax.axis_size(axis))
    route = [(i - distance, i) for i in devices if i - distance in devices]
    return lax.ppermute(block, axis, route)


def rows_at(index):
    return pl.ds(pl.multiple_of(index * BS, BS), BS)


def attend(
    run_blocks,
    scale,
    picks,
    bias_ref,
    q_ref,
    g_ref,
    own_ref,
    low_ref,
    high_ref,
    anchor_ref,
    r0_ref,
    r1_ref,
    r2_ref,
    r3_ref,
    attn_ref,
    dq_ref,
    down_ref,
    dlow_ref,
    dhigh_ref,
    danchor_ref,
    s0_ref,
    s1_ref,
    s2_ref,
    s3_ref,
    frame,
    pool,
    frame_sum,
    anchor_sum,
    pool_sum,
):
    run_rows = run_blocks * BS
    frame[:, :BS] = low_ref[...]
    frame[:, BS : BS + run_rows] = own_ref[...]
    frame[:, BS + run_rows :] = high_ref[...]
    for turn, ref in enumerate((r0_ref, r1_ref, r2_ref, r3_ref)):
        pool[:, turn * run_rows : (turn + 1) * run_rows] = ref[...]
    frame_sum[...] = jnp.zeros_like(frame_sum)
    anchor_sum[...] = jnp.zeros_like(anchor_sum)
    pool_sum[...] = jnp.zeros_like(pool_sum)

    for b in range(run_blocks):
        rows = slice(b * BS, (b + 1) * BS)
        q = q_ref[rows, :]
        g = g_ref[rows, :]
        chosen = [rows_at(picks[b * 3 + slot]) for slot in range(3)]
        k_list, v_list = (
            jnp.concatenate(
                [frame[which, b * BS : (b + 3) * BS, :], anchor_ref[which]]
                + [pool[which, at, :] for at in chosen],
                axis=0,
            )
            for which in (0, 1)
        )
        across = (((1,), (1,)), ((), ()))
        along = (((0,), (0,)), ((), ()))
        logits = lax.dot_general(q, k_list, across, preferred_element_type=jnp.float32)
        grad_probs = lax.dot_general(g, v_list, across, preferred_element_type=jnp.float32)
        logits = logits * scale + bias_ref[b : b + 1, :]
        raw = jnp.exp(logits - jnp.max(logits, axis=1, keepdims=True))
        probs = raw * (1.0 / jnp.sum(raw, axis=1, keepdims=True))
        probs_b = probs.astype(jnp.bfloat16)
        attn = jnp.dot(probs_b, v_list, preferred_element_type=jnp.float32).astype(jnp.bfloat16)
        attn_ref[rows, :] = attn
        delta = jnp.sum(g.astype(jnp.float32) * attn.astype(jnp.float32), axis=1, keepdims=True)
        grad_logits = (probs * (grad_probs - delta)).astype(jnp.bfloat16)
        dq = jnp.dot(grad_logits, k_list, preferred_element_type=jnp.float32)
        dq_ref[rows, :] = (dq * scale).astype(jnp.bfloat16)
        for which, left, right in ((0, grad_logits, q), (1, probs_b, g)):
            parts = lax.dot_general(left, right, along, preferred_element_type=jnp.float32)
            frame_sum[which, b * BS : (b + 3) * BS, :] += parts[: 3 * BS]
            anchor_sum[which] += parts[3 * BS : 4 * BS]
            for slot, at in enumerate(chosen):
                pool_sum[which, at, :] += parts[(4 + slot) * BS : (5 + slot) * BS]

    for which, factor in ((0, scale), (1, 1.0)):
        down_ref[which] = frame_sum[which, BS : BS + run_rows, :] * factor
        dlow_ref[which] = (frame_sum[which, :BS, :] * factor).astype(jnp.bfloat16)
        dhigh_ref[which] = (frame_sum[which, BS + run_rows :, :] * factor).astype(jnp.bfloat16)
        danchor_ref[which] = anchor_sum[which] * factor
        for turn, ref in enumerate((s0_ref, s1_ref, s2_ref, s3_ref)):
            ref[which] = (
                pool_sum[which, turn * run_rows : (turn + 1) * run_rows, :] * factor
            ).astype(jnp.bfloat16)


def attention_both_ways(picks, bias, queries, grad_attention, own, low, high, anchor, arrivals):
    row_count, width_here = queries.shape
    heads_here = width_here // HDIM
    run_blocks = row_count // BS
    flat = pl.BlockSpec((row_count, HDIM), lambda h, p: (0, h))
    run = pl.BlockSpec((2, row_count, HDIM), lambda h, p: (0, 0, h))
    edge = pl.BlockSpec((2, BS, HDIM), lambda h, p: (0, 0, h))
    shape = jax.ShapeDtypeStruct
    flat_shape = shape((row_count, width_here), jnp.bfloat16)
    run_shape = shape((2, row_count, width_here), jnp.bfloat16)
    edge_shape = shape((2, BS, width_here), jnp.bfloat16)
    pairs = row_count * 7 * BS * width_here
    return pl.pallas_call(
        functools.partial(attend, run_blocks, 1.0 / math.sqrt(HDIM)),
        grid_spec=pltpu.PrefetchScalarGridSpec(
            num_scalar_prefetch=1,
            grid=(heads_here,),
            in_specs=[pl.BlockSpec(bias.shape, lambda h, p: (0, 0)), flat, flat, run]
            + [edge] * 3
            + [run] * 4,
            out_specs=[flat, flat, run, edge, edge, edge] + [run] * 4,
            scratch_shapes=[
                pltpu.VMEM((2, row_count + 2 * BS, HDIM), jnp.bfloat16),
                pltpu.VMEM((2, 4 * row_count, HDIM), jnp.bfloat16),
                pltpu.VMEM((2, row_count + 2 * BS, HDIM), jnp.float32),
                pltpu.VMEM((2, BS, HDIM), jnp.float32),
                pltpu.VMEM((2, 4 * row_count, HDIM), jnp.float32),
            ],
        ),
        out_shape=[
            flat_shape,
            flat_shape,
            shape((2, row_count, width_here), jnp.float32),
            edge_shape,
            edge_shape,
            shape((2, BS, width_here), jnp.float32),
        ]
        + [run_shape] * 4,
        cost_estimate=pl.CostEstimate(
            flops=10 * pairs, bytes_accessed=8 * 2**20, transcendentals=pairs // HDIM
        ),
        name="attention_both_ways",
    )(picks, bias, queries, grad_attention, own, low, high, anchor, *arrivals)


def body(queries, keys, values, out_weight, upstream, rand_round, rand_block):
    row_count, width_here = queries.shape
    run_blocks = row_count // BS
    axis_count = lax.axis_size("ctx")
    position = lax.axis_index("ctx")
    offsets = [axis_count * factor // 8 for factor in (4, 2, 3, 5)]
    total_blocks = axis_count * run_blocks
    blocks = position * run_blocks + jnp.arange(run_blocks, dtype=jnp.int32)
    always = jnp.ones((run_blocks,), jnp.bool_)
    allowed = jnp.stack(
        [blocks >= 1, always, blocks <= total_blocks - 2, blocks >= 2, always, always, always],
        axis=1,
    )
    bias = jnp.repeat(jnp.where(allowed, 0.0, -jnp.inf).astype(jnp.float32), BS, axis=1)
    picks = (rand_round * run_blocks + rand_block).reshape(-1)
    key_value = jnp.stack([keys, values])
    low = shifted(key_value[:, -BS:], "ctx", 1)
    high = shifted(key_value[:, :BS], "ctx", -1)
    anchor = spread_down(key_value[:, :BS], "ctx")
    arrivals = [from_behind(key_value, "ctx", offset) for offset in offsets]
    grad_attention = lax.dot_general(
        lax.all_gather(upstream, "head", axis=1, tiled=True),
        out_weight,
        (((1,), (1,)), ((), ())),
        preferred_element_type=jnp.float32,
    ).astype(jnp.bfloat16)
    attention, grad_queries, own_grad, low_grad, high_grad, anchor_grad, *spread = (
        attention_both_ways(
            picks, bias, queries, grad_attention, key_value, low, high, anchor, arrivals
        )
    )
    partial_out = jnp.dot(attention, out_weight, preferred_element_type=jnp.float32)
    mixed = lax.psum_scatter(
        partial_out.astype(jnp.bfloat16), "head", scatter_dimension=1, tiled=True
    )
    anchor_grad = sum_up(anchor_grad, "ctx")
    from_high = shifted(low_grad, "ctx", -1).astype(jnp.float32)
    from_low = shifted(high_grad, "ctx", 1).astype(jnp.float32)
    first = from_low + jnp.where(position == 0, anchor_grad, 0.0)
    for sent, offset in zip(spread, offsets):
        own_grad = own_grad + from_behind(sent, "ctx", -offset).astype(jnp.float32)
    own_grad = jnp.concatenate(
        [
            own_grad[:, :BS] + first,
            own_grad[:, BS:-BS],
            own_grad[:, -BS:] + from_high,
        ],
        axis=1,
    ).astype(jnp.bfloat16)
    return (mixed, grad_queries, own_grad[0], own_grad[1])


def solution(mesh):
    placed = (
        P("ctx", "head"),
        P("ctx", "head"),
        P("ctx", "head"),
        P("head", None),
        P("ctx", "head"),
        P("ctx", None),
        P("ctx", None),
    )
    return jax.shard_map(
        body,
        mesh=mesh,
        in_specs=placed,
        out_specs=(P("ctx", "head"), P("ctx", "head"), P("ctx", "head"), P("ctx", "head")),
        check_vma=False,
    )
```

```python
import functools
import math

import jax
import jax.numpy as jnp
from jax import lax
from jax.experimental import pallas as pl
from jax.experimental.pallas import tpu as pltpu
from jax.sharding import PartitionSpec as P

HDIM = 128
BS = 64


def tree_strides(count, radix=4):
    strides, stride = [], 1
    while stride < count:
        strides.append((stride, min(radix, count // stride)))
        stride *= radix
    return strides


def spread_down(value, axis):
    count = lax.axis_size(axis)
    position = lax.axis_index(axis)
    for stride, ways in reversed(tree_strides(count)):
        digit = (position // stride) % ways
        arrivals = [
            lax.ppermute(
                value, axis, [(i, i + turn * stride) for i in range(0, count, stride * ways)]
            )
            for turn in range(1, ways)
        ]
        holds = position % (stride * ways) == 0
        fresh = arrivals[0]
        for turn in range(2, ways):
            fresh = jnp.where(digit == turn, arrivals[turn - 1], fresh)
        value = jnp.where(holds, value, fresh)
    return value


def sum_stage(value, axis, stride, ways, left):
    sent = value.astype(jnp.bfloat16)
    count = lax.axis_size(axis)
    bases = [i for i in range(count) if (i // stride) % ways == 0 and left(i)]
    for turn in range(1, ways):
        route = [(i + turn * stride, i) for i in bases]
        value = value + lax.ppermute(sent, axis, route).astype(jnp.float32)
    return value


def sum_up(value, axis, held):
    done = []
    strides = tree_strides(lax.axis_size(axis))
    for stride, ways in reversed(strides):
        above = list(done)
        value = sum_stage(
            value, axis, stride, ways, lambda i: all((i // s) % w == 0 for s, w in above)
        )
        done.append((stride, ways))
        if len(done) == len(strides) - 1:
            value, held = lax.optimization_barrier((value, held))
    return value, held


def from_behind(block, axis, distance):
    devices = range(lax.axis_size(axis))
    route = [((i - distance) % len(devices), i) for i in devices]
    return lax.ppermute(block, axis, route)


def shifted(block, axis, distance):
    devices = range(lax.axis_size(axis))
    route = [(i - distance, i) for i in devices if i - distance in devices]
    return lax.ppermute(block, axis, route)


def rows_at(index):
    return pl.ds(pl.multiple_of(index * BS, BS), BS)


def attend(
    run_blocks,
    scale,
    picks,
    bias_ref,
    q_ref,
    g_ref,
    own_ref,
    low_ref,
    high_ref,
    anchor_ref,
    r0_ref,
    r1_ref,
    r2_ref,
    r3_ref,
    attn_ref,
    dq_ref,
    down_ref,
    dlow_ref,
    dhigh_ref,
    danchor_ref,
    s0_ref,
    s1_ref,
    s2_ref,
    s3_ref,
    frame,
    pool,
    frame_sum,
    anchor_sum,
    pool_sum,
):
    run_rows = run_blocks * BS
    frame[:, :BS] = low_ref[...]
    frame[:, BS : BS + run_rows] = own_ref[...]
    frame[:, BS + run_rows :] = high_ref[...]
    for turn, ref in enumerate((r0_ref, r1_ref, r2_ref, r3_ref)):
        pool[:, turn * run_rows : (turn + 1) * run_rows] = ref[...]
    frame_sum[...] = jnp.zeros_like(frame_sum)
    anchor_sum[...] = jnp.zeros_like(anchor_sum)
    pool_sum[...] = jnp.zeros_like(pool_sum)

    for b in range(run_blocks):
        rows = slice(b * BS, (b + 1) * BS)
        q = q_ref[rows, :]
        g = g_ref[rows, :]
        chosen = [rows_at(picks[b * 3 + slot]) for slot in range(3)]
        k_list, v_list = (
            jnp.concatenate(
                [frame[which, b * BS : (b + 3) * BS, :], anchor_ref[which]]
                + [pool[which, at, :] for at in chosen],
                axis=0,
            )
            for which in (0, 1)
        )
        across = (((1,), (1,)), ((), ()))
        along = (((0,), (0,)), ((), ()))
        logits = lax.dot_general(q, k_list, across, preferred_element_type=jnp.float32)
        grad_probs = lax.dot_general(g, v_list, across, preferred_element_type=jnp.float32)
        logits = logits * scale + bias_ref[b : b + 1, :]
        raw = jnp.exp(logits - jnp.max(logits, axis=1, keepdims=True))
        probs = raw * (1.0 / jnp.sum(raw, axis=1, keepdims=True))
        probs_b = probs.astype(jnp.bfloat16)
        attn = jnp.dot(probs_b, v_list, preferred_element_type=jnp.float32).astype(jnp.bfloat16)
        attn_ref[rows, :] = attn
        delta = jnp.sum(g.astype(jnp.float32) * attn.astype(jnp.float32), axis=1, keepdims=True)
        grad_logits = (probs * (grad_probs - delta)).astype(jnp.bfloat16)
        dq = jnp.dot(grad_logits, k_list, preferred_element_type=jnp.float32)
        dq_ref[rows, :] = (dq * scale).astype(jnp.bfloat16)
        for which, left, right in ((0, grad_logits, q), (1, probs_b, g)):
            parts = lax.dot_general(left, right, along, preferred_element_type=jnp.float32)
            frame_sum[which, b * BS : (b + 3) * BS, :] += parts[: 3 * BS]
            anchor_sum[which] += parts[3 * BS : 4 * BS]
            for slot, at in enumerate(chosen):
                pool_sum[which, at, :] += parts[(4 + slot) * BS : (5 + slot) * BS]

    for which, factor in ((0, scale), (1, 1.0)):
        down_ref[which] = frame_sum[which, BS : BS + run_rows, :] * factor
        dlow_ref[which] = (frame_sum[which, :BS, :] * factor).astype(jnp.bfloat16)
        dhigh_ref[which] = (frame_sum[which, BS + run_rows :, :] * factor).astype(jnp.bfloat16)
        danchor_ref[which] = anchor_sum[which] * factor
        for turn, ref in enumerate((s0_ref, s1_ref, s2_ref, s3_ref)):
            ref[which] = (
                pool_sum[which, turn * run_rows : (turn + 1) * run_rows, :] * factor
            ).astype(jnp.bfloat16)


def attention_both_ways(picks, bias, queries, grad_attention, own, low, high, anchor, arrivals):
    row_count, width_here = queries.shape
    heads_here = width_here // HDIM
    run_blocks = row_count // BS
    flat = pl.BlockSpec((row_count, HDIM), lambda h, p: (0, h))
    run = pl.BlockSpec((2, row_count, HDIM), lambda h, p: (0, 0, h))
    edge = pl.BlockSpec((2, BS, HDIM), lambda h, p: (0, 0, h))
    shape = jax.ShapeDtypeStruct
    flat_shape = shape((row_count, width_here), jnp.bfloat16)
    run_shape = shape((2, row_count, width_here), jnp.bfloat16)
    edge_shape = shape((2, BS, width_here), jnp.bfloat16)
    pairs = row_count * 7 * BS * width_here
    return pl.pallas_call(
        functools.partial(attend, run_blocks, 1.0 / math.sqrt(HDIM)),
        grid_spec=pltpu.PrefetchScalarGridSpec(
            num_scalar_prefetch=1,
            grid=(heads_here,),
            in_specs=[pl.BlockSpec(bias.shape, lambda h, p: (0, 0)), flat, flat, run]
            + [edge] * 3
            + [run] * 4,
            out_specs=[flat, flat, run, edge, edge, edge] + [run] * 4,
            scratch_shapes=[
                pltpu.VMEM((2, row_count + 2 * BS, HDIM), jnp.bfloat16),
                pltpu.VMEM((2, 4 * row_count, HDIM), jnp.bfloat16),
                pltpu.VMEM((2, row_count + 2 * BS, HDIM), jnp.float32),
                pltpu.VMEM((2, BS, HDIM), jnp.float32),
                pltpu.VMEM((2, 4 * row_count, HDIM), jnp.float32),
            ],
        ),
        out_shape=[
            flat_shape,
            flat_shape,
            shape((2, row_count, width_here), jnp.float32),
            edge_shape,
            edge_shape,
            shape((2, BS, width_here), jnp.float32),
        ]
        + [run_shape] * 4,
        cost_estimate=pl.CostEstimate(
            flops=10 * pairs, bytes_accessed=8 * 2**20, transcendentals=pairs // HDIM
        ),
        name="attention_both_ways",
    )(picks, bias, queries, grad_attention, own, low, high, anchor, *arrivals)


def body(queries, keys, values, out_weight, upstream, rand_round, rand_block):
    row_count, width_here = queries.shape
    run_blocks = row_count // BS
    axis_count = lax.axis_size("ctx")
    position = lax.axis_index("ctx")
    offsets = [axis_count * factor // 8 for factor in (4, 2, 3, 5)]
    total_blocks = axis_count * run_blocks
    blocks = position * run_blocks + jnp.arange(run_blocks, dtype=jnp.int32)
    always = jnp.ones((run_blocks,), jnp.bool_)
    allowed = jnp.stack(
        [blocks >= 1, always, blocks <= total_blocks - 2, blocks >= 2, always, always, always],
        axis=1,
    )
    bias = jnp.repeat(jnp.where(allowed, 0.0, -jnp.inf).astype(jnp.float32), BS, axis=1)
    picks = (rand_round * run_blocks + rand_block).reshape(-1)
    key_value = jnp.stack([keys, values])
    low = shifted(key_value[:, -BS:], "ctx", 1)
    high = shifted(key_value[:, :BS], "ctx", -1)
    anchor = spread_down(key_value[:, :BS], "ctx")
    arrivals = [from_behind(key_value, "ctx", offset) for offset in offsets]
    grad_attention = lax.dot_general(
        lax.all_gather(upstream, "head", axis=1, tiled=True),
        out_weight,
        (((1,), (1,)), ((), ())),
        preferred_element_type=jnp.float32,
    ).astype(jnp.bfloat16)
    attention, grad_queries, own_grad, low_grad, high_grad, anchor_grad, *spread = (
        attention_both_ways(
            picks, bias, queries, grad_attention, key_value, low, high, anchor, arrivals
        )
    )
    partial_out = jnp.dot(attention, out_weight, preferred_element_type=jnp.float32)
    mixed = lax.psum_scatter(
        partial_out.astype(jnp.bfloat16), "head", scatter_dimension=1, tiled=True
    )
    anchor_grad, held = sum_up(anchor_grad, "ctx", spread[1:])
    spread = [spread[0], *held]
    from_high = shifted(low_grad, "ctx", -1).astype(jnp.float32)
    from_low = shifted(high_grad, "ctx", 1).astype(jnp.float32)
    first = from_low + jnp.where(position == 0, anchor_grad, 0.0)
    for sent, offset in zip(spread, offsets):
        own_grad = own_grad + from_behind(sent, "ctx", -offset).astype(jnp.float32)
    own_grad = jnp.concatenate(
        [
            own_grad[:, :BS] + first,
            own_grad[:, BS:-BS],
            own_grad[:, -BS:] + from_high,
        ],
        axis=1,
    ).astype(jnp.bfloat16)
    return (mixed, grad_queries, own_grad[0], own_grad[1])


def solution(mesh):
    placed = (
        P("ctx", "head"),
        P("ctx", "head"),
        P("ctx", "head"),
        P("head", None),
        P("ctx", "head"),
        P("ctx", None),
        P("ctx", None),
    )
    return jax.shard_map(
        body,
        mesh=mesh,
        in_specs=placed,
        out_specs=(P("ctx", "head"), P("ctx", "head"), P("ctx", "head"), P("ctx", "head")),
        check_vma=False,
    )
```

```python
import functools
import math

import jax
import jax.numpy as jnp
from jax import lax
from jax.experimental import pallas as pl
from jax.experimental.pallas import tpu as pltpu
from jax.sharding import PartitionSpec as P

HDIM = 128
BS = 64


def tree_strides(count, radix=4):
    strides, stride = [], 1
    while stride < count:
        strides.append((stride, min(radix, count // stride)))
        stride *= radix
    return strides


def spread_down(value, axis):
    count = lax.axis_size(axis)
    position = lax.axis_index(axis)
    for stride, ways in reversed(tree_strides(count)):
        digit = (position // stride) % ways
        arrivals = [
            lax.ppermute(
                value, axis, [(i, i + turn * stride) for i in range(0, count, stride * ways)]
            )
            for turn in range(1, ways)
        ]
        holds = position % (stride * ways) == 0
        fresh = arrivals[0]
        for turn in range(2, ways):
            fresh = jnp.where(digit == turn, arrivals[turn - 1], fresh)
        value = jnp.where(holds, value, fresh)
    return value


def sum_up(value, axis, stages):
    count = lax.axis_size(axis)
    for stride, ways in stages:
        sent = value.astype(jnp.bfloat16)
        for turn in range(1, ways):
            route = [(i + turn * stride, i) for i in range(0, count, stride * ways)]
            value = value + lax.ppermute(sent, axis, route).astype(jnp.float32)
    return value


def from_behind(block, axis, distance):
    devices = range(lax.axis_size(axis))
    route = [((i - distance) % len(devices), i) for i in devices]
    return lax.ppermute(block, axis, route)


def shifted(block, axis, distance):
    devices = range(lax.axis_size(axis))
    route = [(i - distance, i) for i in devices if i - distance in devices]
    return lax.ppermute(block, axis, route)


def rows_at(index):
    return pl.ds(pl.multiple_of(index * BS, BS), BS)


def attend(
    run_blocks,
    scale,
    picks,
    bias_ref,
    q_ref,
    g_ref,
    own_ref,
    low_ref,
    high_ref,
    anchor_ref,
    r0_ref,
    r1_ref,
    r2_ref,
    r3_ref,
    attn_ref,
    dq_ref,
    down_ref,
    dlow_ref,
    dhigh_ref,
    danchor_ref,
    s0_ref,
    s1_ref,
    s2_ref,
    s3_ref,
    frame,
    pool,
    frame_sum,
    anchor_sum,
    pool_sum,
):
    run_rows = run_blocks * BS
    frame[:, :BS] = low_ref[...]
    frame[:, BS : BS + run_rows] = own_ref[...]
    frame[:, BS + run_rows :] = high_ref[...]
    for turn, ref in enumerate((r0_ref, r1_ref, r2_ref, r3_ref)):
        pool[:, turn * run_rows : (turn + 1) * run_rows] = ref[...]
    frame_sum[...] = jnp.zeros_like(frame_sum)
    anchor_sum[...] = jnp.zeros_like(anchor_sum)
    pool_sum[...] = jnp.zeros_like(pool_sum)

    for b in range(run_blocks):
        rows = slice(b * BS, (b + 1) * BS)
        q = q_ref[rows, :]
        g = g_ref[rows, :]
        chosen = [rows_at(picks[b * 3 + slot]) for slot in range(3)]
        k_list, v_list = (
            jnp.concatenate(
                [frame[which, b * BS : (b + 3) * BS, :], anchor_ref[which]]
                + [pool[which, at, :] for at in chosen],
                axis=0,
            )
            for which in (0, 1)
        )
        across = (((1,), (1,)), ((), ()))
        along = (((0,), (0,)), ((), ()))
        logits = lax.dot_general(q, k_list, across, preferred_element_type=jnp.float32)
        grad_probs = lax.dot_general(g, v_list, across, preferred_element_type=jnp.float32)
        logits = logits * scale + bias_ref[b : b + 1, :]
        raw = jnp.exp(logits - jnp.max(logits, axis=1, keepdims=True))
        probs = raw * (1.0 / jnp.sum(raw, axis=1, keepdims=True))
        probs_b = probs.astype(jnp.bfloat16)
        attn = jnp.dot(probs_b, v_list, preferred_element_type=jnp.float32).astype(jnp.bfloat16)
        attn_ref[rows, :] = attn
        delta = jnp.sum(g.astype(jnp.float32) * attn.astype(jnp.float32), axis=1, keepdims=True)
        grad_logits = (probs * (grad_probs - delta)).astype(jnp.bfloat16)
        dq = jnp.dot(grad_logits, k_list, preferred_element_type=jnp.float32)
        dq_ref[rows, :] = (dq * scale).astype(jnp.bfloat16)
        for which, left, right in ((0, grad_logits, q), (1, probs_b, g)):
            parts = lax.dot_general(left, right, along, preferred_element_type=jnp.float32)
            frame_sum[which, b * BS : (b + 3) * BS, :] += parts[: 3 * BS]
            anchor_sum[which] += parts[3 * BS : 4 * BS]
            for slot, at in enumerate(chosen):
                pool_sum[which, at, :] += parts[(4 + slot) * BS : (5 + slot) * BS]

    for which, factor in ((0, scale), (1, 1.0)):
        down_ref[which] = frame_sum[which, BS : BS + run_rows, :] * factor
        dlow_ref[which] = (frame_sum[which, :BS, :] * factor).astype(jnp.bfloat16)
        dhigh_ref[which] = (frame_sum[which, BS + run_rows :, :] * factor).astype(jnp.bfloat16)
        danchor_ref[which] = anchor_sum[which] * factor
        for turn, ref in enumerate((s0_ref, s1_ref, s2_ref, s3_ref)):
            ref[which] = (
                pool_sum[which, turn * run_rows : (turn + 1) * run_rows, :] * factor
            ).astype(jnp.bfloat16)


def attention_both_ways(picks, bias, queries, grad_attention, own, low, high, anchor, arrivals):
    row_count, width_here = queries.shape
    heads_here = width_here // HDIM
    run_blocks = row_count // BS
    flat = pl.BlockSpec((row_count, HDIM), lambda h, p: (0, h))
    run = pl.BlockSpec((2, row_count, HDIM), lambda h, p: (0, 0, h))
    edge = pl.BlockSpec((2, BS, HDIM), lambda h, p: (0, 0, h))
    shape = jax.ShapeDtypeStruct
    flat_shape = shape((row_count, width_here), jnp.bfloat16)
    run_shape = shape((2, row_count, width_here), jnp.bfloat16)
    edge_shape = shape((2, BS, width_here), jnp.bfloat16)
    pairs = row_count * 7 * BS * width_here
    return pl.pallas_call(
        functools.partial(attend, run_blocks, 1.0 / math.sqrt(HDIM)),
        grid_spec=pltpu.PrefetchScalarGridSpec(
            num_scalar_prefetch=1,
            grid=(heads_here,),
            in_specs=[pl.BlockSpec(bias.shape, lambda h, p: (0, 0)), flat, flat, run]
            + [edge] * 3
            + [run] * 4,
            out_specs=[flat, flat, run, edge, edge, edge] + [run] * 4,
            scratch_shapes=[
                pltpu.VMEM((2, row_count + 2 * BS, HDIM), jnp.bfloat16),
                pltpu.VMEM((2, 4 * row_count, HDIM), jnp.bfloat16),
                pltpu.VMEM((2, row_count + 2 * BS, HDIM), jnp.float32),
                pltpu.VMEM((2, BS, HDIM), jnp.float32),
                pltpu.VMEM((2, 4 * row_count, HDIM), jnp.float32),
            ],
        ),
        out_shape=[
            flat_shape,
            flat_shape,
            shape((2, row_count, width_here), jnp.float32),
            edge_shape,
            edge_shape,
            shape((2, BS, width_here), jnp.float32),
        ]
        + [run_shape] * 4,
        cost_estimate=pl.CostEstimate(
            flops=10 * pairs, bytes_accessed=8 * 2**20, transcendentals=pairs // HDIM
        ),
        name="attention_both_ways",
    )(picks, bias, queries, grad_attention, own, low, high, anchor, *arrivals)


def body(queries, keys, values, out_weight, upstream, rand_round, rand_block):
    row_count, width_here = queries.shape
    run_blocks = row_count // BS
    axis_count = lax.axis_size("ctx")
    position = lax.axis_index("ctx")
    offsets = [axis_count * factor // 8 for factor in (4, 2, 3, 5)]
    total_blocks = axis_count * run_blocks
    blocks = position * run_blocks + jnp.arange(run_blocks, dtype=jnp.int32)
    always = jnp.ones((run_blocks,), jnp.bool_)
    allowed = jnp.stack(
        [blocks >= 1, always, blocks <= total_blocks - 2, blocks >= 2, always, always, always],
        axis=1,
    )
    bias = jnp.repeat(jnp.where(allowed, 0.0, -jnp.inf).astype(jnp.float32), BS, axis=1)
    picks = (rand_round * run_blocks + rand_block).reshape(-1)
    key_value = jnp.stack([keys, values])
    low = shifted(key_value[:, -BS:], "ctx", 1)
    high = shifted(key_value[:, :BS], "ctx", -1)
    anchor = spread_down(key_value[:, :BS], "ctx")
    arrivals = [from_behind(key_value, "ctx", offsets[0])]
    anchor, held = lax.optimization_barrier((anchor, key_value))
    arrivals += [from_behind(held, "ctx", offset) for offset in offsets[1:]]
    grad_attention = lax.dot_general(
        lax.all_gather(upstream, "head", axis=1, tiled=True),
        out_weight,
        (((1,), (1,)), ((), ())),
        preferred_element_type=jnp.float32,
    ).astype(jnp.bfloat16)
    attention, grad_queries, own_grad, low_grad, high_grad, anchor_grad, *spread = (
        attention_both_ways(
            picks, bias, queries, grad_attention, key_value, low, high, anchor, arrivals
        )
    )
    partial_out = jnp.dot(attention, out_weight, preferred_element_type=jnp.float32)
    mixed = lax.psum_scatter(
        partial_out.astype(jnp.bfloat16), "head", scatter_dimension=1, tiled=True
    )
    returned = [from_behind(sent, "ctx", -offset) for sent, offset in zip(spread, offsets)]
    anchor_grad = sum_up(anchor_grad, "ctx", [(1, 2), (2, 2)])
    anchor_grad, returned = lax.optimization_barrier((anchor_grad, returned))
    anchor_grad = sum_up(anchor_grad, "ctx", tree_strides(axis_count)[1:])
    from_high = shifted(low_grad, "ctx", -1).astype(jnp.float32)
    from_low = shifted(high_grad, "ctx", 1).astype(jnp.float32)
    first = from_low + jnp.where(position == 0, anchor_grad, 0.0)
    for arrived in returned:
        own_grad = own_grad + arrived.astype(jnp.float32)
    own_grad = jnp.concatenate(
        [
            own_grad[:, :BS] + first,
            own_grad[:, BS:-BS],
            own_grad[:, -BS:] + from_high,
        ],
        axis=1,
    ).astype(jnp.bfloat16)
    return (mixed, grad_queries, own_grad[0], own_grad[1])


def solution(mesh):
    placed = (
        P("ctx", "head"),
        P("ctx", "head"),
        P("ctx", "head"),
        P("head", None),
        P("ctx", "head"),
        P("ctx", None),
        P("ctx", None),
    )
    return jax.shard_map(
        body,
        mesh=mesh,
        in_specs=placed,
        out_specs=(P("ctx", "head"), P("ctx", "head"), P("ctx", "head"), P("ctx", "head")),
        check_vma=False,
    )
```

```python
import functools
import math

import jax
import jax.numpy as jnp
from jax import lax
from jax.experimental import pallas as pl
from jax.experimental.pallas import tpu as pltpu
from jax.sharding import PartitionSpec as P

HDIM = 128
BS = 64


def tree_strides(count, radix=4):
    strides, stride = [], 1
    while stride < count:
        strides.append((stride, min(radix, count // stride)))
        stride *= radix
    return strides


def spread_down(value, axis):
    count = lax.axis_size(axis)
    position = lax.axis_index(axis)
    for stride, ways in reversed(tree_strides(count)):
        digit = (position // stride) % ways
        arrivals = [
            lax.ppermute(
                value, axis, [(i, i + turn * stride) for i in range(0, count, stride * ways)]
            )
            for turn in range(1, ways)
        ]
        holds = position % (stride * ways) == 0
        fresh = arrivals[0]
        for turn in range(2, ways):
            fresh = jnp.where(digit == turn, arrivals[turn - 1], fresh)
        value = jnp.where(holds, value, fresh)
    return value


def sum_up(value, axis, stages):
    count = lax.axis_size(axis)
    for stride, ways in stages:
        sent = value.astype(jnp.bfloat16)
        for turn in range(1, ways):
            route = [(i + turn * stride, i) for i in range(0, count, stride * ways)]
            value = value + lax.ppermute(sent, axis, route).astype(jnp.float32)
    return value


def from_behind(block, axis, distance):
    devices = range(lax.axis_size(axis))
    route = [((i - distance) % len(devices), i) for i in devices]
    return lax.ppermute(block, axis, route)


def shifted(block, axis, distance):
    devices = range(lax.axis_size(axis))
    route = [(i - distance, i) for i in devices if i - distance in devices]
    return lax.ppermute(block, axis, route)


def rows_at(index):
    return pl.ds(pl.multiple_of(index * BS, BS), BS)


def attend(
    run_blocks,
    scale,
    picks,
    bias_ref,
    q_ref,
    g_ref,
    own_ref,
    low_ref,
    high_ref,
    anchor_ref,
    r0_ref,
    r1_ref,
    r2_ref,
    r3_ref,
    attn_ref,
    dq_ref,
    down_ref,
    dlow_ref,
    dhigh_ref,
    danchor_ref,
    s0_ref,
    s1_ref,
    s2_ref,
    s3_ref,
    frame,
    pool,
    frame_sum,
    anchor_sum,
    pool_sum,
):
    run_rows = run_blocks * BS
    frame[:, :BS] = low_ref[...]
    frame[:, BS : BS + run_rows] = own_ref[...]
    frame[:, BS + run_rows :] = high_ref[...]
    for turn, ref in enumerate((r0_ref, r1_ref, r2_ref, r3_ref)):
        pool[:, turn * run_rows : (turn + 1) * run_rows] = ref[...]
    frame_sum[...] = jnp.zeros_like(frame_sum)
    anchor_sum[...] = jnp.zeros_like(anchor_sum)
    pool_sum[...] = jnp.zeros_like(pool_sum)

    for b in range(run_blocks):
        rows = slice(b * BS, (b + 1) * BS)
        q = q_ref[rows, :]
        g = g_ref[rows, :]
        chosen = [rows_at(picks[b * 3 + slot]) for slot in range(3)]
        k_list, v_list = (
            jnp.concatenate(
                [frame[which, b * BS : (b + 3) * BS, :], anchor_ref[which]]
                + [pool[which, at, :] for at in chosen],
                axis=0,
            )
            for which in (0, 1)
        )
        across = (((1,), (1,)), ((), ()))
        along = (((0,), (0,)), ((), ()))
        logits = lax.dot_general(q, k_list, across, preferred_element_type=jnp.float32)
        grad_probs = lax.dot_general(g, v_list, across, preferred_element_type=jnp.float32)
        logits = logits * scale + bias_ref[b : b + 1, :]
        raw = jnp.exp(logits - jnp.max(logits, axis=1, keepdims=True))
        probs = raw * (1.0 / jnp.sum(raw, axis=1, keepdims=True))
        probs_b = probs.astype(jnp.bfloat16)
        attn = jnp.dot(probs_b, v_list, preferred_element_type=jnp.float32).astype(jnp.bfloat16)
        attn_ref[rows, :] = attn
        delta = jnp.sum(g.astype(jnp.float32) * attn.astype(jnp.float32), axis=1, keepdims=True)
        grad_logits = (probs * (grad_probs - delta)).astype(jnp.bfloat16)
        dq = jnp.dot(grad_logits, k_list, preferred_element_type=jnp.float32)
        dq_ref[rows, :] = (dq * scale).astype(jnp.bfloat16)
        for which, left, right in ((0, grad_logits, q), (1, probs_b, g)):
            parts = lax.dot_general(left, right, along, preferred_element_type=jnp.float32)
            frame_sum[which, b * BS : (b + 3) * BS, :] += parts[: 3 * BS]
            anchor_sum[which] += parts[3 * BS : 4 * BS]
            for slot, at in enumerate(chosen):
                pool_sum[which, at, :] += parts[(4 + slot) * BS : (5 + slot) * BS]

    for which, factor in ((0, scale), (1, 1.0)):
        down_ref[which] = frame_sum[which, BS : BS + run_rows, :] * factor
        dlow_ref[which] = (frame_sum[which, :BS, :] * factor).astype(jnp.bfloat16)
        dhigh_ref[which] = (frame_sum[which, BS + run_rows :, :] * factor).astype(jnp.bfloat16)
        danchor_ref[which] = anchor_sum[which] * factor
        for turn, ref in enumerate((s0_ref, s1_ref, s2_ref, s3_ref)):
            ref[which] = (
                pool_sum[which, turn * run_rows : (turn + 1) * run_rows, :] * factor
            ).astype(jnp.bfloat16)


def attention_both_ways(picks, bias, queries, grad_attention, own, low, high, anchor, arrivals):
    row_count, width_here = queries.shape
    heads_here = width_here // HDIM
    run_blocks = row_count // BS
    flat = pl.BlockSpec((row_count, HDIM), lambda h, p: (0, h))
    run = pl.BlockSpec((2, row_count, HDIM), lambda h, p: (0, 0, h))
    edge = pl.BlockSpec((2, BS, HDIM), lambda h, p: (0, 0, h))
    shape = jax.ShapeDtypeStruct
    flat_shape = shape((row_count, width_here), jnp.bfloat16)
    run_shape = shape((2, row_count, width_here), jnp.bfloat16)
    edge_shape = shape((2, BS, width_here), jnp.bfloat16)
    pairs = row_count * 7 * BS * width_here
    return pl.pallas_call(
        functools.partial(attend, run_blocks, 1.0 / math.sqrt(HDIM)),
        grid_spec=pltpu.PrefetchScalarGridSpec(
            num_scalar_prefetch=1,
            grid=(heads_here,),
            in_specs=[pl.BlockSpec(bias.shape, lambda h, p: (0, 0)), flat, flat, run]
            + [edge] * 3
            + [run] * 4,
            out_specs=[flat, flat, run, edge, edge, edge] + [run] * 4,
            scratch_shapes=[
                pltpu.VMEM((2, row_count + 2 * BS, HDIM), jnp.bfloat16),
                pltpu.VMEM((2, 4 * row_count, HDIM), jnp.bfloat16),
                pltpu.VMEM((2, row_count + 2 * BS, HDIM), jnp.float32),
                pltpu.VMEM((2, BS, HDIM), jnp.float32),
                pltpu.VMEM((2, 4 * row_count, HDIM), jnp.float32),
            ],
        ),
        out_shape=[
            flat_shape,
            flat_shape,
            shape((2, row_count, width_here), jnp.float32),
            edge_shape,
            edge_shape,
            shape((2, BS, width_here), jnp.float32),
        ]
        + [run_shape] * 4,
        cost_estimate=pl.CostEstimate(
            flops=10 * pairs, bytes_accessed=8 * 2**20, transcendentals=pairs // HDIM
        ),
        name="attention_both_ways",
    )(picks, bias, queries, grad_attention, own, low, high, anchor, *arrivals)


def body(queries, keys, values, out_weight, upstream, rand_round, rand_block):
    row_count, width_here = queries.shape
    run_blocks = row_count // BS
    axis_count = lax.axis_size("ctx")
    position = lax.axis_index("ctx")
    offsets = [axis_count * factor // 8 for factor in (4, 2, 3, 5)]
    total_blocks = axis_count * run_blocks
    blocks = position * run_blocks + jnp.arange(run_blocks, dtype=jnp.int32)
    always = jnp.ones((run_blocks,), jnp.bool_)
    allowed = jnp.stack(
        [blocks >= 1, always, blocks <= total_blocks - 2, blocks >= 2, always, always, always],
        axis=1,
    )
    bias = jnp.repeat(jnp.where(allowed, 0.0, -jnp.inf).astype(jnp.float32), BS, axis=1)
    picks = (rand_round * run_blocks + rand_block).reshape(-1)
    key_value = jnp.stack([keys, values])
    low = shifted(key_value[:, -BS:], "ctx", 1)
    high = shifted(key_value[:, :BS], "ctx", -1)
    anchor = spread_down(key_value[:, :BS], "ctx")
    arrivals = [from_behind(key_value, "ctx", offset) for offset in offsets]
    grad_attention = lax.dot_general(
        lax.all_gather(upstream, "head", axis=1, tiled=True),
        out_weight,
        (((1,), (1,)), ((), ())),
        preferred_element_type=jnp.float32,
    ).astype(jnp.bfloat16)
    attention, grad_queries, own_grad, low_grad, high_grad, anchor_grad, *spread = (
        attention_both_ways(
            picks, bias, queries, grad_attention, key_value, low, high, anchor, arrivals
        )
    )
    partial_out = jnp.dot(attention, out_weight, preferred_element_type=jnp.float32)
    mixed = lax.psum_scatter(
        partial_out.astype(jnp.bfloat16), "head", scatter_dimension=1, tiled=True
    )
    returned = [from_behind(sent, "ctx", -offset) for sent, offset in zip(spread, offsets)]
    anchor_grad = sum_up(anchor_grad, "ctx", [(1, 2), (2, 2)])
    anchor_grad, returned = lax.optimization_barrier((anchor_grad, returned))
    anchor_grad = sum_up(anchor_grad, "ctx", tree_strides(axis_count)[1:])
    from_high = shifted(low_grad, "ctx", -1).astype(jnp.float32)
    from_low = shifted(high_grad, "ctx", 1).astype(jnp.float32)
    first = from_low + jnp.where(position == 0, anchor_grad, 0.0)
    for arrived in returned:
        own_grad = own_grad + arrived.astype(jnp.float32)
    own_grad = jnp.concatenate(
        [
            own_grad[:, :BS] + first,
            own_grad[:, BS:-BS],
            own_grad[:, -BS:] + from_high,
        ],
        axis=1,
    ).astype(jnp.bfloat16)
    return (mixed, grad_queries, own_grad[0], own_grad[1])


def solution(mesh):
    placed = (
        P("ctx", "head"),
        P("ctx", "head"),
        P("ctx", "head"),
        P("head", None),
        P("ctx", "head"),
        P("ctx", None),
        P("ctx", None),
    )
    return jax.shard_map(
        body,
        mesh=mesh,
        in_specs=placed,
        out_specs=(P("ctx", "head"), P("ctx", "head"), P("ctx", "head"), P("ctx", "head")),
        check_vma=False,
    )
```

```python
import functools
import math

import jax
import jax.numpy as jnp
from jax import lax
from jax.experimental import pallas as pl
from jax.experimental.pallas import tpu as pltpu
from jax.sharding import PartitionSpec as P

HDIM = 128
BS = 64


def tree_strides(count, radix=4):
    strides, stride = [], 1
    while stride < count:
        strides.append((stride, min(radix, count // stride)))
        stride *= radix
    return strides


def spread_down(value, axis, stages):
    position = lax.axis_index(axis)
    for stride, ways in stages:
        arrivals = [
            lax.ppermute(value, axis, [(i, i + turn * stride) for i in range(stride)])
            for turn in range(1, ways)
        ]
        fresh = arrivals[0]
        for turn in range(2, ways):
            fresh = jnp.where(position // stride == turn, arrivals[turn - 1], fresh)
        value = jnp.where(position < stride, value, fresh)
    return value


def sum_up(value, axis, stages):
    count = lax.axis_size(axis)
    for stride, ways in stages:
        sent = value.astype(jnp.bfloat16)
        for turn in range(1, ways):
            route = [(i + turn * stride, i) for i in range(0, count, stride * ways)]
            value = value + lax.ppermute(sent, axis, route).astype(jnp.float32)
    return value


def from_behind(block, axis, distance):
    devices = range(lax.axis_size(axis))
    route = [((i - distance) % len(devices), i) for i in devices]
    return lax.ppermute(block, axis, route)


def shifted(block, axis, distance):
    devices = range(lax.axis_size(axis))
    route = [(i - distance, i) for i in devices if i - distance in devices]
    return lax.ppermute(block, axis, route)


def rows_at(index):
    return pl.ds(pl.multiple_of(index * BS, BS), BS)


def attend(
    run_blocks,
    scale,
    picks,
    bias_ref,
    q_ref,
    g_ref,
    own_ref,
    low_ref,
    high_ref,
    anchor_ref,
    r0_ref,
    r1_ref,
    r2_ref,
    r3_ref,
    attn_ref,
    dq_ref,
    down_ref,
    dlow_ref,
    dhigh_ref,
    danchor_ref,
    s0_ref,
    s1_ref,
    s2_ref,
    s3_ref,
    frame,
    pool,
    frame_sum,
    anchor_sum,
    pool_sum,
):
    run_rows = run_blocks * BS
    frame[:, :BS] = low_ref[...]
    frame[:, BS : BS + run_rows] = own_ref[...]
    frame[:, BS + run_rows :] = high_ref[...]
    for turn, ref in enumerate((r0_ref, r1_ref, r2_ref, r3_ref)):
        pool[:, turn * run_rows : (turn + 1) * run_rows] = ref[...]
    frame_sum[...] = jnp.zeros_like(frame_sum)
    anchor_sum[...] = jnp.zeros_like(anchor_sum)
    pool_sum[...] = jnp.zeros_like(pool_sum)

    for b in range(run_blocks):
        rows = slice(b * BS, (b + 1) * BS)
        q = q_ref[rows, :]
        g = g_ref[rows, :]
        chosen = [rows_at(picks[b * 3 + slot]) for slot in range(3)]
        k_list, v_list = (
            jnp.concatenate(
                [frame[which, b * BS : (b + 3) * BS, :], anchor_ref[which]]
                + [pool[which, at, :] for at in chosen],
                axis=0,
            )
            for which in (0, 1)
        )
        across = (((1,), (1,)), ((), ()))
        along = (((0,), (0,)), ((), ()))
        logits = lax.dot_general(q, k_list, across, preferred_element_type=jnp.float32)
        grad_probs = lax.dot_general(g, v_list, across, preferred_element_type=jnp.float32)
        logits = logits * scale + bias_ref[b : b + 1, :]
        raw = jnp.exp(logits - jnp.max(logits, axis=1, keepdims=True))
        probs = raw * (1.0 / jnp.sum(raw, axis=1, keepdims=True))
        probs_b = probs.astype(jnp.bfloat16)
        attn = jnp.dot(probs_b, v_list, preferred_element_type=jnp.float32).astype(jnp.bfloat16)
        attn_ref[rows, :] = attn
        delta = jnp.sum(g.astype(jnp.float32) * attn.astype(jnp.float32), axis=1, keepdims=True)
        grad_logits = (probs * (grad_probs - delta)).astype(jnp.bfloat16)
        dq = jnp.dot(grad_logits, k_list, preferred_element_type=jnp.float32)
        dq_ref[rows, :] = (dq * scale).astype(jnp.bfloat16)
        for which, left, right in ((0, grad_logits, q), (1, probs_b, g)):
            parts = lax.dot_general(left, right, along, preferred_element_type=jnp.float32)
            frame_sum[which, b * BS : (b + 3) * BS, :] += parts[: 3 * BS]
            anchor_sum[which] += parts[3 * BS : 4 * BS]
            for slot, at in enumerate(chosen):
                pool_sum[which, at, :] += parts[(4 + slot) * BS : (5 + slot) * BS]

    for which, factor in ((0, scale), (1, 1.0)):
        down_ref[which] = frame_sum[which, BS : BS + run_rows, :] * factor
        dlow_ref[which] = (frame_sum[which, :BS, :] * factor).astype(jnp.bfloat16)
        dhigh_ref[which] = (frame_sum[which, BS + run_rows :, :] * factor).astype(jnp.bfloat16)
        danchor_ref[which] = anchor_sum[which] * factor
        for turn, ref in enumerate((s0_ref, s1_ref, s2_ref, s3_ref)):
            ref[which] = (
                pool_sum[which, turn * run_rows : (turn + 1) * run_rows, :] * factor
            ).astype(jnp.bfloat16)


def attention_both_ways(picks, bias, queries, grad_attention, own, low, high, anchor, arrivals):
    row_count, width_here = queries.shape
    heads_here = width_here // HDIM
    run_blocks = row_count // BS
    flat = pl.BlockSpec((row_count, HDIM), lambda h, p: (0, h))
    run = pl.BlockSpec((2, row_count, HDIM), lambda h, p: (0, 0, h))
    edge = pl.BlockSpec((2, BS, HDIM), lambda h, p: (0, 0, h))
    shape = jax.ShapeDtypeStruct
    flat_shape = shape((row_count, width_here), jnp.bfloat16)
    run_shape = shape((2, row_count, width_here), jnp.bfloat16)
    edge_shape = shape((2, BS, width_here), jnp.bfloat16)
    pairs = row_count * 7 * BS * width_here
    return pl.pallas_call(
        functools.partial(attend, run_blocks, 1.0 / math.sqrt(HDIM)),
        grid_spec=pltpu.PrefetchScalarGridSpec(
            num_scalar_prefetch=1,
            grid=(heads_here,),
            in_specs=[pl.BlockSpec(bias.shape, lambda h, p: (0, 0)), flat, flat, run]
            + [edge] * 3
            + [run] * 4,
            out_specs=[flat, flat, run, edge, edge, edge] + [run] * 4,
            scratch_shapes=[
                pltpu.VMEM((2, row_count + 2 * BS, HDIM), jnp.bfloat16),
                pltpu.VMEM((2, 4 * row_count, HDIM), jnp.bfloat16),
                pltpu.VMEM((2, row_count + 2 * BS, HDIM), jnp.float32),
                pltpu.VMEM((2, BS, HDIM), jnp.float32),
                pltpu.VMEM((2, 4 * row_count, HDIM), jnp.float32),
            ],
        ),
        out_shape=[
            flat_shape,
            flat_shape,
            shape((2, row_count, width_here), jnp.float32),
            edge_shape,
            edge_shape,
            shape((2, BS, width_here), jnp.float32),
        ]
        + [run_shape] * 4,
        cost_estimate=pl.CostEstimate(
            flops=10 * pairs, bytes_accessed=8 * 2**20, transcendentals=pairs // HDIM
        ),
        name="attention_both_ways",
    )(picks, bias, queries, grad_attention, own, low, high, anchor, *arrivals)


def body(queries, keys, values, out_weight, upstream, rand_round, rand_block):
    row_count, width_here = queries.shape
    run_blocks = row_count // BS
    axis_count = lax.axis_size("ctx")
    position = lax.axis_index("ctx")
    offsets = [axis_count * factor // 8 for factor in (4, 2, 3, 5)]
    total_blocks = axis_count * run_blocks
    blocks = position * run_blocks + jnp.arange(run_blocks, dtype=jnp.int32)
    always = jnp.ones((run_blocks,), jnp.bool_)
    allowed = jnp.stack(
        [blocks >= 1, always, blocks <= total_blocks - 2, blocks >= 2, always, always, always],
        axis=1,
    )
    bias = jnp.repeat(jnp.where(allowed, 0.0, -jnp.inf).astype(jnp.float32), BS, axis=1)
    picks = (rand_round * run_blocks + rand_block).reshape(-1)
    key_value = jnp.stack([keys, values])
    low = shifted(key_value[:, -BS:], "ctx", 1)
    high = shifted(key_value[:, :BS], "ctx", -1)
    arrivals = [from_behind(key_value, "ctx", offset) for offset in offsets]
    anchor = spread_down(key_value[:, :BS], "ctx", [(1, 2), (2, 2)])
    anchor, arrivals = lax.optimization_barrier((anchor, arrivals))
    anchor = spread_down(anchor, "ctx", tree_strides(axis_count)[1:])
    grad_attention = lax.dot_general(
        lax.all_gather(upstream, "head", axis=1, tiled=True),
        out_weight,
        (((1,), (1,)), ((), ())),
        preferred_element_type=jnp.float32,
    ).astype(jnp.bfloat16)
    attention, grad_queries, own_grad, low_grad, high_grad, anchor_grad, *spread = (
        attention_both_ways(
            picks, bias, queries, grad_attention, key_value, low, high, anchor, arrivals
        )
    )
    partial_out = jnp.dot(attention, out_weight, preferred_element_type=jnp.float32)
    mixed = lax.psum_scatter(
        partial_out.astype(jnp.bfloat16), "head", scatter_dimension=1, tiled=True
    )
    returned = [from_behind(sent, "ctx", -offset) for sent, offset in zip(spread, offsets)]
    anchor_grad = sum_up(anchor_grad, "ctx", [(1, 2), (2, 2)])
    anchor_grad, returned = lax.optimization_barrier((anchor_grad, returned))
    anchor_grad = sum_up(anchor_grad, "ctx", tree_strides(axis_count)[1:])
    from_high = shifted(low_grad, "ctx", -1).astype(jnp.float32)
    from_low = shifted(high_grad, "ctx", 1).astype(jnp.float32)
    first = from_low + jnp.where(position == 0, anchor_grad, 0.0)
    for arrived in returned:
        own_grad = own_grad + arrived.astype(jnp.float32)
    own_grad = jnp.concatenate(
        [
            own_grad[:, :BS] + first,
            own_grad[:, BS:-BS],
            own_grad[:, -BS:] + from_high,
        ],
        axis=1,
    ).astype(jnp.bfloat16)
    return (mixed, grad_queries, own_grad[0], own_grad[1])


def solution(mesh):
    placed = (
        P("ctx", "head"),
        P("ctx", "head"),
        P("ctx", "head"),
        P("head", None),
        P("ctx", "head"),
        P("ctx", None),
        P("ctx", None),
    )
    return jax.shard_map(
        body,
        mesh=mesh,
        in_specs=placed,
        out_specs=(P("ctx", "head"), P("ctx", "head"), P("ctx", "head"), P("ctx", "head")),
        check_vma=False,
    )
```
